128 devices in a mesh: ctx: 32 (over y, z, core), exp: 4 (over x).
Axes of the slice: x: 4, y: 4, z: 4, core: 2. Of those that a mesh axis runs over, the one named last changes fastest.
Arguments:
- stream_in: bfloat16 [4096, 6144], P('ctx'), may hold values from -41 to 41
- queries: bfloat16 [4096, 8192], P('ctx', 'exp'), may hold values from -6 to 6
- key_proj: bfloat16 [4096, 8192], P('ctx', 'exp'), may hold values from -0.5390625 to 0.5390625
- values: bfloat16 [4096, 8192], P('ctx', 'exp'), may hold values from -6 to 6
- attn_gate: bfloat16 [4096, 8192], P('ctx', 'exp'), may hold values from -6 to 6
- decay_rates: float32 [64], P('exp'), may hold values from 1.2207031e-05 to 0.05
- attn_gain: float32 [8192], P('exp'), may hold values from 0.25 to 1.75
- out_weight: bfloat16 [8192, 6144], P('exp', 'ctx'), may hold values from -0.0625 to 0.0625
- ffn_gain: float32 [6144], replicated, may hold values from 0.25 to 1.75
- routing: int32 [4096, 2], P('ctx'), may hold values from 0 to 31, as said below
- route_weights: float32 [4096, 2], P('ctx'), may hold values from 0.25 to 1
- w_gate: bfloat16 [4, 6144, 9216], P('exp', None, 'ctx'), may hold values from -0.078125 to 0.078125
- w_up: bfloat16 [4, 6144, 9216], P('exp', None, 'ctx'), may hold values from -0.078125 to 0.078125
- w_down: bfloat16 [4, 9216, 6144], P('exp', 'ctx'), may hold values from -0.0625 to 0.0625
Outputs:
- residual_out: bfloat16 [4096, 6144], P(('ctx', 'exp'))
- expert_out: bfloat16 [32, 4, 8, 6144], P('ctx', 'exp')
The draws below stay inside these ranges and needn't reach their ends.
Inputs may be any that keep to these rules, and one draw needn't show every extreme that they name: `routing`: the two ids of a row differ and at most one of them is below 4. In each aligned block of 128 rows (one context shard) an id below 4 is named by at most 8 rows; one such id, the same for all blocks, is named by exactly 8 rows in every block.
All inputs are finite; a program needn't handle non-finite values.
Results may differ from the reference program's by a relative error of at most 0.025.
Values may be sent and summed in bfloat16 or wider, within the bound.
A program may use at most 128 MiB of HBM per device.

```python
import math
import jax
import jax.numpy as jnp
from jax import lax

D = 6144
HEADS = 64
DH = 128
FF = 9216
ROUTED = 32
TOPK = 2
TOK = 128
SEQ = 4096
EXPERTS = 4
CAP = 8
N_CTX = 32
N_EXP = 4


def draw_stream_in(key, part):
    key_base, key_rows, key_cols = jax.random.split(key, 3)
    base_values = jnp.clip(jax.random.normal(key_base, (SEQ, D), jnp.float32), -4.0, 4.0)
    row_scale = jnp.exp(jax.random.uniform(key_rows, (SEQ, 1), jnp.float32, -1.15, 1.15))
    col_scale = jnp.exp(jax.random.uniform(key_cols, (1, D), jnp.float32, -1.15, 1.15))
    return (base_values * row_scale * col_scale).astype(jnp.bfloat16)


def draw_decay_rates(key, part):
    key_kind, key_slow, key_fast = jax.random.split(key, 3)
    slow_heads = jax.random.randint(key_kind, (HEADS,), 0, 2) > 0
    slow_rate = jnp.exp(math.log(0.05 / SEQ) + jax.random.uniform(key_slow, (HEADS,), jnp.float32) * math.log(20.0))
    fast_rate = jnp.exp(math.log(0.02) + jax.random.uniform(key_fast, (HEADS,), jnp.float32) * math.log(2.5))
    return jnp.where(slow_heads, slow_rate, fast_rate)


def draw_routing(key, part):
    key_full, key_counts, key_order, key_other, key_step, key_swap = jax.random.split(key, 6)
    full_expert = jax.random.randint(key_full, (), 0, EXPERTS)
    slot_counts = jax.random.randint(key_counts, (N_CTX, EXPERTS), 1, CAP // 2 + 1)
    slot_counts = jnp.where(jnp.arange(EXPERTS)[None, :] == full_expert, CAP, slot_counts)
    shuffle_order = jax.vmap(lambda one_key: jax.random.permutation(one_key, TOK))(jax.random.split(key_order, N_CTX))
    inverse_order = jnp.argsort(shuffle_order, axis=1, stable=True)
    slot_position = jnp.arange(TOK, dtype=jnp.int32)
    slot_owner = slot_position // CAP
    slot_within = slot_position % CAP
    owner_clipped = jnp.minimum(slot_owner, EXPERTS - 1)
    slot_limit = slot_counts[:, owner_clipped]
    slot_live = (slot_owner[None, :] < EXPERTS) & (slot_within[None, :] < slot_limit)
    held_grid = jnp.where(slot_live, slot_owner[None, :], -1)
    token_held = jnp.take_along_axis(held_grid, inverse_order, axis=1).reshape(SEQ)
    other_first = jax.random.randint(key_other, (SEQ,), EXPERTS, ROUTED)
    other_second = EXPERTS + (other_first - EXPERTS + jax.random.randint(key_step, (SEQ,), 1, ROUTED - EXPERTS)) % (ROUTED - EXPERTS)
    first_id = jnp.where(token_held >= 0, token_held, other_first)
    swap_flag = jax.random.randint(key_swap, (SEQ,), 0, 2)
    column_zero = jnp.where(swap_flag == 1, other_second, first_id)
    column_one = jnp.where(swap_flag == 1, first_id, other_second)
    return jnp.stack([column_zero, column_one], axis=1).astype(jnp.int32)


def levels(own_key, dims, cuts, least, largest):
    def one(dim, shards_of):
        steps = jax.random.uniform(jax.random.fold_in(jax.random.fold_in(own_key, 6), dim), (shards_of,), jnp.float32, least / len(cuts), largest / len(cuts))
        return jnp.repeat(jnp.exp(steps), dims[dim] // shards_of).reshape((-1,) + (1,) * (len(dims) - dim - 1))

    gain = one(*cuts[0])
    for cut in cuts[1:]:
        gain = gain * one(*cut)
    return gain


def scatter_about(stream_key, extent, width, most, shards=(), kind=jnp.bfloat16):
    array = jax.random.normal(stream_key, extent, jnp.float32) * width
    if len(shards) > 0:
        array = levels(stream_key, extent, shards, -0.22, 0.18) * array
    return jnp.clip(array, min=-most, max=most).astype(kind)


def setup_inputs(seed: int = 0) -> dict:
    streams_of = jax.random.split(jax.random.key(seed), 15)
    return {
        "stream_in": draw_stream_in(jax.random.fold_in(streams_of[14], 71), 0),
        "queries": scatter_about(streams_of[1], (SEQ, HEADS * DH), 1.0, 6.0, ((0, 32), (1, 4))),
        "key_proj": scatter_about(streams_of[2], (SEQ, HEADS * DH), 0.09, 0.5390625, ((0, 32), (1, 4))),
        "values": scatter_about(streams_of[3], (SEQ, HEADS * DH), 1.0, 6.0, ((0, 32), (1, 4))),
        "attn_gate": scatter_about(streams_of[4], (SEQ, HEADS * DH), 1.0, 6.0, ((0, 32), (1, 4))),
        "decay_rates": draw_decay_rates(jax.random.fold_in(streams_of[14], 71), 0),
        "attn_gain": jnp.clip(1.0 + 0.15 * jax.random.normal(streams_of[6], (HEADS * DH,), jnp.float32), 0.25, 1.75),
        "out_weight": scatter_about(streams_of[7], (HEADS * DH, D), (HEADS * DH) ** -0.5, 0.0625, ((0, 4), (1, 32))),
        "ffn_gain": jnp.clip(1.0 + 0.15 * jax.random.normal(streams_of[8], (D,), jnp.float32), 0.25, 1.75),
        "routing": draw_routing(jax.random.fold_in(streams_of[14], 71), 0),
        "route_weights": jnp.clip(0.25 + 0.75 * jax.random.uniform(streams_of[10], (SEQ, TOPK), jnp.float32) ** levels(streams_of[10], (SEQ, TOPK), ((0, 32),), -0.2, 0.2), 0.25, 1.0),
        "w_gate": scatter_about(streams_of[11], (EXPERTS, D, FF), D ** -0.5, 0.078125, ((0, 4), (2, 32))),
        "w_up": scatter_about(streams_of[12], (EXPERTS, D, FF), D ** -0.5, 0.078125, ((0, 4), (2, 32))),
        "w_down": scatter_about(streams_of[13], (EXPERTS, FF, D), FF ** -0.5, 0.0625, ((0, 4), (1, 32))),
    }


HIGHEST = lax.Precision.HIGHEST

def lightning(queries, key_proj, values, decay_rates):
    query_blocks = queries.reshape(N_CTX, TOK, HEADS, DH)
    key_blocks = key_proj.reshape(N_CTX, TOK, HEADS, DH)
    value_blocks = values.reshape(N_CTX, TOK, HEADS, DH)
    position = jnp.arange(TOK).astype(jnp.float32)
    distance = position[:, None] - position[None, :]
    decay_mask = jnp.where(distance[None] >= 0.0, jnp.exp(-decay_rates[:, None, None] * jnp.maximum(distance, 0.0)[None]), 0.0)
    lead_decay = jnp.exp(-decay_rates[None, :] * (position + 1.0)[:, None])
    tail_decay = jnp.exp(-decay_rates[None, :] * (TOK - 1.0 - position)[:, None])
    span_decay = jnp.exp(-decay_rates * TOK)

    def advance(carry_state, pieces):
        query_rows, key_rows, value_rows = pieces
        query_wide = query_rows.astype(jnp.float32)
        key_wide = key_rows.astype(jnp.float32)
        value_wide = value_rows.astype(jnp.float32)
        scores = jnp.einsum('ihd,jhd->hij', query_wide, key_wide)
        rounded = lax.optimization_barrier((scores * decay_mask).astype(jnp.bfloat16))
        near_part = jnp.einsum('hij,jhd->ihd', rounded.astype(jnp.float32), value_wide)
        far_part = jnp.einsum('ihd,hde->ihe', query_wide * lead_decay[:, :, None], carry_state, precision=HIGHEST)
        fresh_state = jnp.einsum('jhd,jhe->hde', key_wide * tail_decay[:, :, None], value_wide, precision=HIGHEST)
        return (span_decay[:, None, None] * carry_state + fresh_state, near_part + far_part)
    start_state = jnp.zeros((HEADS, DH, DH), jnp.float32)
    _, attended = lax.scan(advance, start_state, (query_blocks, key_blocks, value_blocks))
    return attended.reshape(N_CTX * TOK, HEADS, DH)

def reference(stream_in, queries, key_proj, values, attn_gate, decay_rates, attn_gain, out_weight, ffn_gain, routing, route_weights, w_gate, w_up, w_down):
    attended = lightning(queries, key_proj, values, decay_rates)
    inverse = lax.rsqrt(lax.optimization_barrier(jnp.mean(attended * attended, axis=2, keepdims=True)) + 1e-06)
    normed = (attended * inverse).reshape(SEQ, HEADS * DH)
    mixed_heads = (normed * attn_gain[None, :] * jax.nn.sigmoid(attn_gate.astype(jnp.float32))).astype(jnp.bfloat16)
    group_width = HEADS // N_EXP * DH
    projected = jnp.zeros((SEQ, D), jnp.float32)
    for group_index in range(N_EXP):
        part_rows = jnp.dot(mixed_heads[:, group_index * group_width:(group_index + 1) * group_width], out_weight[group_index * group_width:(group_index + 1) * group_width], preferred_element_type=jnp.float32)
        projected = projected + lax.optimization_barrier(part_rows.astype(jnp.bfloat16)).astype(jnp.float32)
    residual_out = (stream_in.astype(jnp.float32) + projected).astype(jnp.bfloat16)
    held_ids = jnp.arange(EXPERTS, dtype=jnp.int32)
    route_blocks = routing.reshape(N_CTX, TOK, TOPK)
    hit_mask = route_blocks[..., None] == held_ids
    member = lax.optimization_barrier(jnp.sum(hit_mask.astype(jnp.int32), axis=2)).astype(jnp.int32)
    slot_rank = (jnp.cumsum(member, axis=1) - 1).astype(jnp.int32)
    pick_mask = (member[..., None] == 1) & (slot_rank[..., None] == jnp.arange(CAP, dtype=jnp.int32))
    gate_of = lax.optimization_barrier(jnp.sum(jnp.where(hit_mask, route_weights.reshape(N_CTX, TOK, TOPK)[..., None], 0.0), axis=2))
    slot_weight = lax.optimization_barrier(jnp.sum(jnp.where(pick_mask, gate_of[..., None], 0.0), axis=1))
    slot_hidden = jnp.einsum('ctes,ctd->cesd', pick_mask.astype(jnp.float32), residual_out.reshape(N_CTX, TOK, D).astype(jnp.float32))
    slot_scale = lax.rsqrt(lax.optimization_barrier(jnp.mean(slot_hidden * slot_hidden, axis=3, keepdims=True)) + 1e-06)
    slot_inputs = (slot_hidden * slot_scale * ffn_gain).astype(jnp.bfloat16)
    group_hidden = FF // N_CTX
    outputs = []
    for expert_index in range(EXPERTS):
        expert_rows = slot_inputs[:, expert_index].reshape(N_CTX * CAP, D)
        gate_part = jnp.dot(expert_rows, w_gate[expert_index], preferred_element_type=jnp.float32)
        up_part = jnp.dot(expert_rows, w_up[expert_index], preferred_element_type=jnp.float32)
        activated = (jax.nn.silu(gate_part) * up_part).astype(jnp.bfloat16)
        act_groups = activated.reshape(N_CTX * CAP, N_CTX, group_hidden).transpose(1, 0, 2)
        down_groups = w_down[expert_index].reshape(N_CTX, group_hidden, D)

        def accumulate(running, pieces):
            act_rows, down_rows = pieces
            part_rows = jnp.dot(act_rows, down_rows, preferred_element_type=jnp.float32)
            return (running + lax.optimization_barrier(part_rows.astype(jnp.bfloat16)).astype(jnp.float32), None)
        summed_down, _ = lax.scan(accumulate, jnp.zeros((N_CTX * CAP, D), jnp.float32), (act_groups, down_groups))
        outputs.append(summed_down.reshape(N_CTX, CAP, D))
    totals = jnp.stack(outputs, axis=1)
    expert_out = (totals * slot_weight[..., None]).astype(jnp.bfloat16)
    return (residual_out, expert_out)
```

```python
import jax
import jax.numpy as jnp
from jax import lax
from jax.sharding import PartitionSpec as P

HIGHEST = lax.Precision.HIGHEST


def decayed_prefix(local_state, decay_rates, rows_here):
    count = lax.axis_size("ctx")

    def shift(value, step):
        pairs = [(i, i + step) for i in range(count - step)]
        return lax.ppermute(value.astype(jnp.bfloat16), "ctx", pairs).astype(jnp.float32)

    running = shift(local_state, 1)
    step = 1
    while step < count:
        factor = jnp.exp(-decay_rates * (rows_here * step))
        running = running + factor[:, None, None] * shift(running, step)
        step *= 2
    return running


def normalize_rows(row_block, ffn_gain):
    wide_rows = row_block.astype(jnp.float32)
    inverse = lax.rsqrt(jnp.mean(wide_rows * wide_rows, axis=1, keepdims=True) + 1e-06)
    return (wide_rows * inverse * ffn_gain[None, :]).astype(jnp.bfloat16)


def per_device(
    stream_in,
    queries,
    key_proj,
    values,
    attn_gate,
    decay_rates,
    attn_gain,
    out_weight,
    ffn_gain,
    routing,
    route_weights,
    w_gate,
    w_up,
    w_down,
):
    rows_here, model_width = stream_in.shape
    head_count = decay_rates.shape[0]
    head_size = queries.shape[1] // head_count
    exp_count = lax.axis_size("exp")
    own_index = lax.axis_index("exp")
    capacity = rows_here // 16
    own_rows = rows_here // exp_count
    per_block = own_rows + capacity
    query_heads = queries.reshape(rows_here, head_count, head_size)
    key_heads = key_proj.reshape(rows_here, head_count, head_size)
    value_heads = values.reshape(rows_here, head_count, head_size)
    positions = jnp.arange(rows_here, dtype=jnp.float32)
    tail_decay = jnp.exp(-decay_rates[None, :] * (rows_here - 1.0 - positions)[:, None])
    weighted_keys = key_heads.astype(jnp.float32) * tail_decay[:, :, None]
    local_state = jnp.einsum(
        "jhd,jhe->hde", weighted_keys, value_heads.astype(jnp.float32), precision=HIGHEST
    )
    prior_state = decayed_prefix(local_state, decay_rates, rows_here)
    scores = jnp.einsum("ihd,jhd->hij", query_heads, key_heads, preferred_element_type=jnp.float32)
    distance = positions[:, None] - positions[None, :]
    decay_mask = jnp.where(
        distance[None] >= 0.0,
        jnp.exp(-decay_rates[:, None, None] * jnp.maximum(distance, 0.0)[None]),
        0.0,
    )
    near_weights = (scores * decay_mask).astype(jnp.bfloat16)
    near_part = jnp.einsum(
        "hij,jhd->ihd", near_weights, value_heads, preferred_element_type=jnp.float32
    )
    lead_decay = jnp.exp(-decay_rates[None, :] * (positions + 1.0)[:, None])
    far_part = jnp.einsum(
        "ihd,hde->ihe",
        query_heads.astype(jnp.float32) * lead_decay[:, :, None],
        prior_state,
        precision=HIGHEST,
    )
    attended = near_part + far_part
    inverse = lax.rsqrt(jnp.mean(attended * attended, axis=2, keepdims=True) + 1e-06)
    normed = (attended * inverse).reshape(rows_here, head_count * head_size)
    mixed_heads = (
        normed * attn_gain[None, :] * jax.nn.sigmoid(attn_gate.astype(jnp.float32))
    ).astype(jnp.bfloat16)
    held_ids = jnp.arange(exp_count, dtype=jnp.int32)
    hit_mask = routing[:, :, None] == held_ids[None, None, :]
    member = jnp.sum(hit_mask.astype(jnp.int32), axis=1)
    gate_of = jnp.sum(jnp.where(hit_mask, route_weights[:, :, None], 0.0), axis=1)
    slot_rank = jnp.cumsum(member, axis=0) - 1
    slot_index = jnp.arange(capacity, dtype=jnp.int32)
    pick_mask = (member[:, :, None] == 1) & (slot_rank[:, :, None] == slot_index[None, None, :])
    selector = pick_mask.reshape(rows_here, exp_count * capacity).T.astype(jnp.bfloat16)
    slot_weight = jnp.sum(jnp.where(pick_mask, gate_of[:, :, None], 0.0), axis=0)
    slot_mixed = jnp.dot(selector, mixed_heads, preferred_element_type=jnp.float32).astype(
        jnp.bfloat16
    )
    row_blocks = jnp.concatenate(
        [mixed_heads.reshape(exp_count, own_rows, -1), slot_mixed.reshape(exp_count, capacity, -1)],
        axis=1,
    )
    stacked = row_blocks.reshape(exp_count * per_block, head_count * head_size)
    partial_rows = jnp.dot(
        stacked,
        lax.all_gather(out_weight, "ctx", axis=1, tiled=True),
        preferred_element_type=jnp.float32,
    )
    partial_term = partial_rows.reshape(1, exp_count, per_block, model_width)
    summed = lax.psum_scatter(
        partial_term.astype(jnp.bfloat16), "exp", scatter_dimension=1, tiled=True
    ).astype(jnp.float32)
    projected = summed.reshape(per_block, model_width)
    stream_own = lax.dynamic_slice_in_dim(stream_in, own_index * own_rows, own_rows, 0)
    own_selector = lax.dynamic_slice_in_dim(selector, own_index * capacity, capacity, 0)
    stream_slots = jnp.dot(own_selector, stream_in, preferred_element_type=jnp.float32)
    residual_rows = jnp.concatenate([stream_own.astype(jnp.float32), stream_slots], axis=0)
    hidden_rows = (residual_rows + projected).astype(jnp.bfloat16)
    residual_out = hidden_rows[:own_rows]
    slot_hidden = hidden_rows[own_rows:]
    outgoing = normalize_rows(slot_hidden, ffn_gain)
    row_piece = lax.all_gather(outgoing, "ctx", axis=0, tiled=True)
    gate_part = jnp.dot(row_piece, w_gate[0], preferred_element_type=jnp.float32)
    up_part = jnp.dot(row_piece, w_up[0], preferred_element_type=jnp.float32)
    activated = (jax.nn.silu(gate_part) * up_part).astype(jnp.bfloat16)
    summed_down = lax.psum_scatter(
        jnp.dot(activated, w_down[0], preferred_element_type=jnp.float32).astype(jnp.bfloat16),
        "ctx",
        scatter_dimension=0,
        tiled=True,
    ).astype(jnp.float32)
    own_weight = lax.dynamic_index_in_dim(slot_weight, own_index, 0, keepdims=False)
    expert_out = (
        (summed_down * own_weight[:, None])
        .astype(jnp.bfloat16)
        .reshape(1, 1, capacity, model_width)
    )
    return (residual_out, expert_out)


def solution(mesh):
    return jax.shard_map(
        per_device,
        mesh=mesh,
        in_specs=(
            P("ctx", None),
            P("ctx", "exp"),
            P("ctx", "exp"),
            P("ctx", "exp"),
            P("ctx", "exp"),
            P("exp"),
            P("exp"),
            P("exp", "ctx"),
            P(),
            P("ctx", None),
            P("ctx", None),
            P("exp", None, "ctx"),
            P("exp", None, "ctx"),
            P("exp", "ctx", None),
        ),
        out_specs=(P(("ctx", "exp"), None), P("ctx", "exp", None, None)),
        check_vma=False,
    )
```

```python
import jax
import jax.numpy as jnp
from jax import lax
from jax.sharding import PartitionSpec as P

HIGHEST = lax.Precision.HIGHEST


def decayed_prefix(local_state, decay_rates, rows_here):
    count = lax.axis_size("ctx")

    def shift(value, step):
        pairs = [(i, i + step) for i in range(count - step)]
        return lax.ppermute(value.astype(jnp.bfloat16), "ctx", pairs).astype(jnp.float32)

    running = shift(local_state, 1)
    step = 1
    while step < count:
        factor = jnp.exp(-decay_rates * (rows_here * step))
        running = running + factor[:, None, None] * shift(running, step)
        step *= 2
    return running


def normalize_rows(row_block, ffn_gain):
    wide_rows = row_block.astype(jnp.float32)
    inverse = lax.rsqrt(jnp.mean(wide_rows * wide_rows, axis=1, keepdims=True) + 1e-06)
    return (wide_rows * inverse * ffn_gain[None, :]).astype(jnp.bfloat16)


def per_device(
    stream_in,
    queries,
    key_proj,
    values,
    attn_gate,
    decay_rates,
    attn_gain,
    out_weight,
    ffn_gain,
    routing,
    route_weights,
    w_gate,
    w_up,
    w_down,
):
    rows_here, model_width = stream_in.shape
    head_count = decay_rates.shape[0]
    head_size = queries.shape[1] // head_count
    exp_count = lax.axis_size("exp")
    own_index = lax.axis_index("exp")
    capacity = rows_here // 16
    own_rows = rows_here // exp_count
    per_block = own_rows + capacity
    query_heads = queries.reshape(rows_here, head_count, head_size)
    key_heads = key_proj.reshape(rows_here, head_count, head_size)
    value_heads = values.reshape(rows_here, head_count, head_size)
    positions = jnp.arange(rows_here, dtype=jnp.float32)
    tail_decay = jnp.exp(-decay_rates[None, :] * (rows_here - 1.0 - positions)[:, None])
    weighted_keys = key_heads.astype(jnp.float32) * tail_decay[:, :, None]
    local_state = jnp.einsum(
        "jhd,jhe->hde", weighted_keys, value_heads.astype(jnp.float32), precision=HIGHEST
    )
    prior_state = decayed_prefix(local_state, decay_rates, rows_here)
    scores = jnp.einsum("ihd,jhd->hij", query_heads, key_heads, preferred_element_type=jnp.float32)
    distance = positions[:, None] - positions[None, :]
    decay_mask = jnp.where(
        distance[None] >= 0.0,
        jnp.exp(-decay_rates[:, None, None] * jnp.maximum(distance, 0.0)[None]),
        0.0,
    )
    near_weights = (scores * decay_mask).astype(jnp.bfloat16)
    near_part = jnp.einsum(
        "hij,jhd->ihd", near_weights, value_heads, preferred_element_type=jnp.float32
    )
    lead_decay = jnp.exp(-decay_rates[None, :] * (positions + 1.0)[:, None])
    far_part = jnp.einsum(
        "ihd,hde->ihe",
        query_heads.astype(jnp.float32) * lead_decay[:, :, None],
        prior_state,
        precision=HIGHEST,
    )
    attended = near_part + far_part
    inverse = lax.rsqrt(jnp.mean(attended * attended, axis=2, keepdims=True) + 1e-06)
    normed = (attended * inverse).reshape(rows_here, head_count * head_size)
    mixed_heads = (
        normed * attn_gain[None, :] * jax.nn.sigmoid(attn_gate.astype(jnp.float32))
    ).astype(jnp.bfloat16)
    held_ids = jnp.arange(exp_count, dtype=jnp.int32)
    hit_mask = routing[:, :, None] == held_ids[None, None, :]
    member = jnp.sum(hit_mask.astype(jnp.int32), axis=1)
    gate_of = jnp.sum(jnp.where(hit_mask, route_weights[:, :, None], 0.0), axis=1)
    slot_rank = jnp.cumsum(member, axis=0) - 1
    slot_index = jnp.arange(capacity, dtype=jnp.int32)
    pick_mask = (member[:, :, None] == 1) & (slot_rank[:, :, None] == slot_index[None, None, :])
    selector = pick_mask.reshape(rows_here, exp_count * capacity).T.astype(jnp.bfloat16)
    slot_weight = jnp.sum(jnp.where(pick_mask, gate_of[:, :, None], 0.0), axis=0)
    slot_mixed = jnp.dot(selector, mixed_heads, preferred_element_type=jnp.float32).astype(
        jnp.bfloat16
    )
    row_blocks = jnp.concatenate(
        [mixed_heads.reshape(exp_count, own_rows, -1), slot_mixed.reshape(exp_count, capacity, -1)],
        axis=1,
    )
    stacked = row_blocks.reshape(exp_count * per_block, head_count * head_size)
    partial_rows = jnp.dot(
        stacked,
        lax.all_gather(out_weight, "ctx", axis=1, tiled=True),
        preferred_element_type=jnp.float32,
    )
    partial_term = partial_rows.reshape(1, exp_count, per_block, model_width)
    swapped = lax.all_to_all(
        partial_term.astype(jnp.bfloat16), "exp", 1, 0, tiled=True
    )
    projected = jnp.sum(swapped.astype(jnp.float32), axis=0).reshape(per_block, model_width)
    stream_own = lax.dynamic_slice_in_dim(stream_in, own_index * own_rows, own_rows, 0)
    own_selector = lax.dynamic_slice_in_dim(selector, own_index * capacity, capacity, 0)
    stream_slots = jnp.dot(own_selector, stream_in, preferred_element_type=jnp.float32)
    residual_rows = jnp.concatenate([stream_own.astype(jnp.float32), stream_slots], axis=0)
    hidden_rows = (residual_rows + projected).astype(jnp.bfloat16)
    residual_out = hidden_rows[:own_rows]
    slot_hidden = hidden_rows[own_rows:]
    outgoing = normalize_rows(slot_hidden, ffn_gain)
    ctx_count = lax.axis_size("ctx")
    row_piece = lax.all_to_all(
        jnp.broadcast_to(outgoing[None], (ctx_count,) + outgoing.shape), "ctx", 0, 0, tiled=True
    ).reshape(ctx_count * capacity, model_width)
    gate_part = jnp.dot(row_piece, w_gate[0], preferred_element_type=jnp.float32)
    up_part = jnp.dot(row_piece, w_up[0], preferred_element_type=jnp.float32)
    activated = (jax.nn.silu(gate_part) * up_part).astype(jnp.bfloat16)
    down_part = jnp.dot(activated, w_down[0], preferred_element_type=jnp.float32)
    down_blocks = lax.all_to_all(
        down_part.astype(jnp.bfloat16).reshape(ctx_count, capacity, model_width), "ctx", 0, 0, tiled=True
    )
    summed_down = jnp.sum(down_blocks.astype(jnp.float32), axis=0)
    own_weight = lax.dynamic_index_in_dim(slot_weight, own_index, 0, keepdims=False)
    expert_out = (
        (summed_down * own_weight[:, None])
        .astype(jnp.bfloat16)
        .reshape(1, 1, capacity, model_width)
    )
    return (residual_out, expert_out)


def solution(mesh):
    return jax.shard_map(
        per_device,
        mesh=mesh,
        in_specs=(
            P("ctx", None),
            P("ctx", "exp"),
            P("ctx", "exp"),
            P("ctx", "exp"),
            P("ctx", "exp"),
            P("exp"),
            P("exp"),
            P("exp", "ctx"),
            P(),
            P("ctx", None),
            P("ctx", None),
            P("exp", None, "ctx"),
            P("exp", None, "ctx"),
            P("exp", "ctx", None),
        ),
        out_specs=(P(("ctx", "exp"), None), P("ctx", "exp", None, None)),
        check_vma=False,
    )
```

```python
import jax
import jax.numpy as jnp
from jax import lax
from jax.sharding import PartitionSpec as P

HIGHEST = lax.Precision.HIGHEST
CTX = ("yz", "core")


def decayed_prefix(local_state, decay_rates, rows_here):
    count = lax.axis_size(CTX)

    def shift(value, step):
        pairs = [(i, i + step) for i in range(count - step)]
        return lax.ppermute(value.astype(jnp.bfloat16), CTX, pairs).astype(jnp.float32)

    running = shift(local_state, 1)
    step = 1
    while step < count:
        factor = jnp.exp(-decay_rates * (rows_here * step))
        running = running + factor[:, None, None] * shift(running, step)
        step *= 2
    return running


def normalize_rows(row_block, ffn_gain):
    wide_rows = row_block.astype(jnp.float32)
    inverse = lax.rsqrt(jnp.mean(wide_rows * wide_rows, axis=1, keepdims=True) + 1e-06)
    return (wide_rows * inverse * ffn_gain[None, :]).astype(jnp.bfloat16)


def per_device(
    stream_in,
    queries,
    key_proj,
    values,
    attn_gate,
    decay_rates,
    attn_gain,
    out_weight,
    ffn_gain,
    routing,
    route_weights,
    w_gate,
    w_up,
    w_down,
):
    rows_here, model_width = stream_in.shape
    head_count = decay_rates.shape[0]
    head_size = queries.shape[1] // head_count
    exp_count = lax.axis_size("exp")
    own_index = lax.axis_index("exp")
    capacity = rows_here // 16
    own_rows = rows_here // exp_count
    per_block = own_rows + capacity
    query_heads = queries.reshape(rows_here, head_count, head_size)
    key_heads = key_proj.reshape(rows_here, head_count, head_size)
    value_heads = values.reshape(rows_here, head_count, head_size)
    positions = jnp.arange(rows_here, dtype=jnp.float32)
    tail_decay = jnp.exp(-decay_rates[None, :] * (rows_here - 1.0 - positions)[:, None])
    weighted_keys = key_heads.astype(jnp.float32) * tail_decay[:, :, None]
    local_state = jnp.einsum(
        "jhd,jhe->hde", weighted_keys, value_heads.astype(jnp.float32), precision=HIGHEST
    )
    prior_state = decayed_prefix(local_state, decay_rates, rows_here)
    scores = jnp.einsum("ihd,jhd->hij", query_heads, key_heads, preferred_element_type=jnp.float32)
    distance = positions[:, None] - positions[None, :]
    decay_mask = jnp.where(
        distance[None] >= 0.0,
        jnp.exp(-decay_rates[:, None, None] * jnp.maximum(distance, 0.0)[None]),
        0.0,
    )
    near_weights = (scores * decay_mask).astype(jnp.bfloat16)
    near_part = jnp.einsum(
        "hij,jhd->ihd", near_weights, value_heads, preferred_element_type=jnp.float32
    )
    lead_decay = jnp.exp(-decay_rates[None, :] * (positions + 1.0)[:, None])
    far_part = jnp.einsum(
        "ihd,hde->ihe",
        query_heads.astype(jnp.float32) * lead_decay[:, :, None],
        prior_state,
        precision=HIGHEST,
    )
    attended = near_part + far_part
    inverse = lax.rsqrt(jnp.mean(attended * attended, axis=2, keepdims=True) + 1e-06)
    normed = (attended * inverse).reshape(rows_here, head_count * head_size)
    mixed_heads = (
        normed * attn_gain[None, :] * jax.nn.sigmoid(attn_gate.astype(jnp.float32))
    ).astype(jnp.bfloat16)
    held_ids = jnp.arange(exp_count, dtype=jnp.int32)
    hit_mask = routing[:, :, None] == held_ids[None, None, :]
    member = jnp.sum(hit_mask.astype(jnp.int32), axis=1)
    gate_of = jnp.sum(jnp.where(hit_mask, route_weights[:, :, None], 0.0), axis=1)
    slot_rank = jnp.cumsum(member, axis=0) - 1
    slot_index = jnp.arange(capacity, dtype=jnp.int32)
    pick_mask = (member[:, :, None] == 1) & (slot_rank[:, :, None] == slot_index[None, None, :])
    selector = pick_mask.reshape(rows_here, exp_count * capacity).T.astype(jnp.bfloat16)
    slot_weight = jnp.sum(jnp.where(pick_mask, gate_of[:, :, None], 0.0), axis=0)
    slot_mixed = jnp.dot(selector, mixed_heads, preferred_element_type=jnp.float32).astype(
        jnp.bfloat16
    )
    row_blocks = jnp.concatenate(
        [mixed_heads.reshape(exp_count, own_rows, -1), slot_mixed.reshape(exp_count, capacity, -1)],
        axis=1,
    )
    stacked = row_blocks.reshape(exp_count * per_block, head_count * head_size)
    pair_rows = lax.all_gather(stacked, "core", axis=0, tiled=True)
    half_weight = lax.all_gather(out_weight, "yz", axis=1, tiled=True)
    half_width = half_weight.shape[1]
    partial_rows = jnp.dot(pair_rows, half_weight, preferred_element_type=jnp.float32)
    partial_term = partial_rows.astype(jnp.bfloat16).reshape(2, exp_count, per_block, half_width)
    swapped = lax.all_to_all(partial_term, "exp", 1, 1, tiled=True)
    head_sum = jnp.sum(swapped.astype(jnp.float32), axis=1)
    by_parity = lax.all_to_all(head_sum, "core", 0, 0, tiled=True)
    block_width = out_weight.shape[1]
    projected = (
        by_parity.reshape(2, per_block, half_width // block_width, block_width)
        .transpose(1, 2, 0, 3)
        .reshape(per_block, model_width)
    )
    stream_own = lax.dynamic_slice_in_dim(stream_in, own_index * own_rows, own_rows, 0)
    own_selector = lax.dynamic_slice_in_dim(selector, own_index * capacity, capacity, 0)
    stream_slots = jnp.dot(own_selector, stream_in, preferred_element_type=jnp.float32)
    residual_rows = jnp.concatenate([stream_own.astype(jnp.float32), stream_slots], axis=0)
    hidden_rows = (residual_rows + projected).astype(jnp.bfloat16)
    residual_out = hidden_rows[:own_rows]
    slot_hidden = hidden_rows[own_rows:]
    outgoing = normalize_rows(slot_hidden, ffn_gain)
    ctx_count = lax.axis_size(CTX)
    row_piece = lax.all_gather(outgoing, CTX, axis=0, tiled=True)
    gate_part = jnp.dot(row_piece, w_gate[0], preferred_element_type=jnp.float32)
    up_part = jnp.dot(row_piece, w_up[0], preferred_element_type=jnp.float32)
    activated = (jax.nn.silu(gate_part) * up_part).astype(jnp.bfloat16)
    down_part = jnp.dot(activated, w_down[0], preferred_element_type=jnp.float32)
    down_blocks = lax.all_to_all(
        down_part.astype(jnp.bfloat16).reshape(ctx_count, capacity, model_width), CTX, 0, 0, tiled=True
    )
    summed_down = jnp.sum(down_blocks.astype(jnp.float32), axis=0)
    own_weight = lax.dynamic_index_in_dim(slot_weight, own_index, 0, keepdims=False)
    expert_out = (
        (summed_down * own_weight[:, None])
        .astype(jnp.bfloat16)
        .reshape(1, 1, capacity, model_width)
    )
    return (residual_out, expert_out)


def solution(mesh):
    ctx_size, exp_size = mesh.devices.shape
    split = jax.sharding.Mesh(mesh.devices.reshape(ctx_size // 2, 2, exp_size), ("yz", "core", "exp"))
    return jax.shard_map(
        per_device,
        mesh=split,
        in_specs=(
            P(CTX, None),
            P(CTX, "exp"),
            P(CTX, "exp"),
            P(CTX, "exp"),
            P(CTX, "exp"),
            P("exp"),
            P("exp"),
            P("exp", CTX),
            P(),
            P(CTX, None),
            P(CTX, None),
            P("exp", None, CTX),
            P("exp", None, CTX),
            P("exp", CTX, None),
        ),
        out_specs=(P((CTX[0], CTX[1], "exp"), None), P(CTX, "exp", None, None)),
        check_vma=False,
    )
```

```python
import jax
import jax.numpy as jnp
from jax import lax
from jax.sharding import PartitionSpec as P

HIGHEST = lax.Precision.HIGHEST
CTX = ("yz", "core")


def decayed_prefix(local_state, decay_rates, rows_here):
    count = lax.axis_size(CTX)

    def shift(value, step):
        pairs = [(i, i + step) for i in range(count - step)]
        return lax.ppermute(value.astype(jnp.bfloat16), CTX, pairs).astype(jnp.float32)

    running = shift(local_state, 1)
    step = 1
    while step < count:
        factor = jnp.exp(-decay_rates * (rows_here * step))
        running = running + factor[:, None, None] * shift(running, step)
        step *= 2
    return running


def partner(value):
    return lax.ppermute(value, "core", [(0, 1), (1, 0)])


def by_core(mine, theirs):
    first = lax.axis_index("core") == 0
    return jnp.where(first, mine, theirs), jnp.where(first, theirs, mine)


def normalize_rows(row_block, ffn_gain):
    wide_rows = row_block.astype(jnp.float32)
    inverse = lax.rsqrt(jnp.mean(wide_rows * wide_rows, axis=1, keepdims=True) + 1e-06)
    return (wide_rows * inverse * ffn_gain[None, :]).astype(jnp.bfloat16)


def per_device(
    stream_in,
    queries,
    key_proj,
    values,
    attn_gate,
    decay_rates,
    attn_gain,
    out_weight,
    ffn_gain,
    routing,
    route_weights,
    w_gate,
    w_up,
    w_down,
):
    rows_here, model_width = stream_in.shape
    head_count = decay_rates.shape[0]
    head_size = queries.shape[1] // head_count
    exp_count = lax.axis_size("exp")
    own_index = lax.axis_index("exp")
    capacity = rows_here // 16
    own_rows = rows_here // exp_count
    per_block = own_rows + capacity
    query_heads = queries.reshape(rows_here, head_count, head_size)
    key_heads = key_proj.reshape(rows_here, head_count, head_size)
    value_heads = values.reshape(rows_here, head_count, head_size)
    positions = jnp.arange(rows_here, dtype=jnp.float32)
    tail_decay = jnp.exp(-decay_rates[None, :] * (rows_here - 1.0 - positions)[:, None])
    weighted_keys = key_heads.astype(jnp.float32) * tail_decay[:, :, None]
    local_state = jnp.einsum(
        "jhd,jhe->hde", weighted_keys, value_heads.astype(jnp.float32), precision=HIGHEST
    )
    prior_state = decayed_prefix(local_state, decay_rates, rows_here)
    scores = jnp.einsum("ihd,jhd->hij", query_heads, key_heads, preferred_element_type=jnp.float32)
    distance = positions[:, None] - positions[None, :]
    decay_mask = jnp.where(
        distance[None] >= 0.0,
        jnp.exp(-decay_rates[:, None, None] * jnp.maximum(distance, 0.0)[None]),
        0.0,
    )
    near_weights = (scores * decay_mask).astype(jnp.bfloat16)
    near_part = jnp.einsum(
        "hij,jhd->ihd", near_weights, value_heads, preferred_element_type=jnp.float32
    )
    lead_decay = jnp.exp(-decay_rates[None, :] * (positions + 1.0)[:, None])
    far_part = jnp.einsum(
        "ihd,hde->ihe",
        query_heads.astype(jnp.float32) * lead_decay[:, :, None],
        prior_state,
        precision=HIGHEST,
    )
    attended = near_part + far_part
    inverse = lax.rsqrt(jnp.mean(attended * attended, axis=2, keepdims=True) + 1e-06)
    normed = (attended * inverse).reshape(rows_here, head_count * head_size)
    mixed_heads = (
        normed * attn_gain[None, :] * jax.nn.sigmoid(attn_gate.astype(jnp.float32))
    ).astype(jnp.bfloat16)
    held_ids = jnp.arange(exp_count, dtype=jnp.int32)
    hit_mask = routing[:, :, None] == held_ids[None, None, :]
    member = jnp.sum(hit_mask.astype(jnp.int32), axis=1)
    gate_of = jnp.sum(jnp.where(hit_mask, route_weights[:, :, None], 0.0), axis=1)
    slot_rank = jnp.cumsum(member, axis=0) - 1
    slot_index = jnp.arange(capacity, dtype=jnp.int32)
    pick_mask = (member[:, :, None] == 1) & (slot_rank[:, :, None] == slot_index[None, None, :])
    selector = pick_mask.reshape(rows_here, exp_count * capacity).T.astype(jnp.bfloat16)
    slot_weight = jnp.sum(jnp.where(pick_mask, gate_of[:, :, None], 0.0), axis=0)
    slot_mixed = jnp.dot(selector, mixed_heads, preferred_element_type=jnp.float32).astype(
        jnp.bfloat16
    )
    row_blocks = jnp.concatenate(
        [mixed_heads.reshape(exp_count, own_rows, -1), slot_mixed.reshape(exp_count, capacity, -1)],
        axis=1,
    )
    stacked = row_blocks.reshape(exp_count * per_block, head_count * head_size)
    pair_rows = jnp.concatenate(by_core(stacked, partner(stacked)), axis=0)
    half_weight = lax.all_gather(out_weight, "yz", axis=1, tiled=True)
    half_width = half_weight.shape[1]
    partial_rows = jnp.dot(pair_rows, half_weight, preferred_element_type=jnp.float32)
    partial_term = partial_rows.astype(jnp.bfloat16).reshape(2, exp_count, per_block, half_width)
    swapped = lax.all_to_all(partial_term, "exp", 1, 1, tiled=True)
    head_sum = jnp.sum(swapped.astype(jnp.float32), axis=1)
    core_here = lax.axis_index("core")
    kept = lax.dynamic_index_in_dim(head_sum, core_here, 0, keepdims=False)
    sent = lax.dynamic_index_in_dim(head_sum, 1 - core_here, 0, keepdims=False)
    by_parity = jnp.stack(by_core(kept, partner(sent)), axis=0)
    block_width = out_weight.shape[1]
    projected = (
        by_parity.reshape(2, per_block, half_width // block_width, block_width)
        .transpose(1, 2, 0, 3)
        .reshape(per_block, model_width)
    )
    stream_own = lax.dynamic_slice_in_dim(stream_in, own_index * own_rows, own_rows, 0)
    own_selector = lax.dynamic_slice_in_dim(selector, own_index * capacity, capacity, 0)
    stream_slots = jnp.dot(own_selector, stream_in, preferred_element_type=jnp.float32)
    residual_rows = jnp.concatenate([stream_own.astype(jnp.float32), stream_slots], axis=0)
    hidden_rows = (residual_rows + projected).astype(jnp.bfloat16)
    residual_out = hidden_rows[:own_rows]
    slot_hidden = hidden_rows[own_rows:]
    outgoing = normalize_rows(slot_hidden, ffn_gain)
    ctx_count = lax.axis_size(CTX)
    chip_rows = jnp.concatenate(by_core(outgoing, partner(outgoing)), axis=0)
    row_piece = lax.all_gather(chip_rows, "yz", axis=0, tiled=True)
    gate_part = jnp.dot(row_piece, w_gate[0], preferred_element_type=jnp.float32)
    up_part = jnp.dot(row_piece, w_up[0], preferred_element_type=jnp.float32)
    activated = (jax.nn.silu(gate_part) * up_part).astype(jnp.bfloat16)
    down_part = jnp.dot(activated, w_down[0], preferred_element_type=jnp.float32)
    down_rows = down_part.astype(jnp.bfloat16).reshape(ctx_count // 2, 2, capacity, model_width)
    down_kept = lax.dynamic_index_in_dim(down_rows, core_here, 1, keepdims=False)
    down_sent = lax.dynamic_index_in_dim(down_rows, 1 - core_here, 1, keepdims=False)
    pair_sum = down_kept.astype(jnp.float32) + partner(down_sent).astype(jnp.float32)
    down_blocks = lax.all_to_all(pair_sum.astype(jnp.bfloat16), "yz", 0, 0, tiled=True)
    summed_down = jnp.sum(down_blocks.astype(jnp.float32), axis=0)
    own_weight = lax.dynamic_index_in_dim(slot_weight, own_index, 0, keepdims=False)
    expert_out = (
        (summed_down * own_weight[:, None])
        .astype(jnp.bfloat16)
        .reshape(1, 1, capacity, model_width)
    )
    return (residual_out, expert_out)


def solution(mesh):
    ctx_size, exp_size = mesh.devices.shape
    split = jax.sharding.Mesh(mesh.devices.reshape(ctx_size // 2, 2, exp_size), ("yz", "core", "exp"))
    return jax.shard_map(
        per_device,
        mesh=split,
        in_specs=(
            P(CTX, None),
            P(CTX, "exp"),
            P(CTX, "exp"),
            P(CTX, "exp"),
            P(CTX, "exp"),
            P("exp"),
            P("exp"),
            P("exp", CTX),
            P(),
            P(CTX, None),
            P(CTX, None),
            P("exp", None, CTX),
            P("exp", None, CTX),
            P("exp", CTX, None),
        ),
        out_specs=(P((CTX[0], CTX[1], "exp"), None), P(CTX, "exp", None, None)),
        check_vma=False,
    )
```

```python
import jax
import jax.numpy as jnp
from jax import lax
from jax.sharding import PartitionSpec as P

HIGHEST = lax.Precision.HIGHEST
CTX = ("yz", "core")


def partner(value):
    return lax.ppermute(value, "core", [(0, 1), (1, 0)])


def by_core(mine, theirs):
    first = lax.axis_index("core") == 0
    return jnp.where(first, mine, theirs), jnp.where(first, theirs, mine)


def decayed_prefix(local_state, decay_rates, rows_here):
    chips = lax.axis_size("yz")
    core_here = lax.axis_index("core")
    half = local_state.shape[0] // 2
    span = jnp.exp(-decay_rates * rows_here)
    other = partner(local_state)
    first_state, second_state = by_core(local_state, other)
    chip_state = span[:, None, None] * first_state + second_state
    my_rates = lax.dynamic_slice_in_dim(decay_rates, core_here * half, half, 0)
    running = lax.dynamic_slice_in_dim(chip_state, core_here * half, half, 0)

    def shift(value, step):
        pairs = [(i, i + step) for i in range(chips - step)]
        return lax.ppermute(value.astype(jnp.bfloat16), "yz", pairs).astype(jnp.float32)

    running = shift(running, 1)
    step = 1
    while step < chips:
        factor = jnp.exp(-my_rates * (2 * rows_here * step))
        running = running + factor[:, None, None] * shift(running, step)
        step *= 2
    mine, theirs = running, partner(running)
    low, high = by_core(mine, theirs)
    chip_prefix = jnp.concatenate([low, high], axis=0)
    return jnp.where(core_here == 0, chip_prefix, span[:, None, None] * chip_prefix + first_state)


def normalize_rows(row_block, ffn_gain):
    wide_rows = row_block.astype(jnp.float32)
    inverse = lax.rsqrt(jnp.mean(wide_rows * wide_rows, axis=1, keepdims=True) + 1e-06)
    return (wide_rows * inverse * ffn_gain[None, :]).astype(jnp.bfloat16)


def per_device(
    stream_in,
    queries,
    key_proj,
    values,
    attn_gate,
    decay_rates,
    attn_gain,
    out_weight,
    ffn_gain,
    routing,
    route_weights,
    w_gate,
    w_up,
    w_down,
):
    rows_here, model_width = stream_in.shape
    head_count = decay_rates.shape[0]
    head_size = queries.shape[1] // head_count
    exp_count = lax.axis_size("exp")
    own_index = lax.axis_index("exp")
    capacity = rows_here // 16
    own_rows = rows_here // exp_count
    per_block = own_rows + capacity
    query_heads = queries.reshape(rows_here, head_count, head_size)
    key_heads = key_proj.reshape(rows_here, head_count, head_size)
    value_heads = values.reshape(rows_here, head_count, head_size)
    positions = jnp.arange(rows_here, dtype=jnp.float32)
    tail_decay = jnp.exp(-decay_rates[None, :] * (rows_here - 1.0 - positions)[:, None])
    weighted_keys = key_heads.astype(jnp.float32) * tail_decay[:, :, None]
    local_state = jnp.einsum(
        "jhd,jhe->hde", weighted_keys, value_heads.astype(jnp.float32), precision=HIGHEST
    )
    prior_state = decayed_prefix(local_state, decay_rates, rows_here)
    scores = jnp.einsum("ihd,jhd->hij", query_heads, key_heads, preferred_element_type=jnp.float32)
    distance = positions[:, None] - positions[None, :]
    decay_mask = jnp.where(
        distance[None] >= 0.0,
        jnp.exp(-decay_rates[:, None, None] * jnp.maximum(distance, 0.0)[None]),
        0.0,
    )
    near_weights = (scores * decay_mask).astype(jnp.bfloat16)
    near_part = jnp.einsum(
        "hij,jhd->ihd", near_weights, value_heads, preferred_element_type=jnp.float32
    )
    lead_decay = jnp.exp(-decay_rates[None, :] * (positions + 1.0)[:, None])
    far_part = jnp.einsum(
        "ihd,hde->ihe",
        query_heads.astype(jnp.float32) * lead_decay[:, :, None],
        prior_state,
        precision=HIGHEST,
    )
    attended = near_part + far_part
    inverse = lax.rsqrt(jnp.mean(attended * attended, axis=2, keepdims=True) + 1e-06)
    normed = (attended * inverse).reshape(rows_here, head_count * head_size)
    mixed_heads = (
        normed * attn_gain[None, :] * jax.nn.sigmoid(attn_gate.astype(jnp.float32))
    ).astype(jnp.bfloat16)
    held_ids = jnp.arange(exp_count, dtype=jnp.int32)
    hit_mask = routing[:, :, None] == held_ids[None, None, :]
    member = jnp.sum(hit_mask.astype(jnp.int32), axis=1)
    gate_of = jnp.sum(jnp.where(hit_mask, route_weights[:, :, None], 0.0), axis=1)
    slot_rank = jnp.cumsum(member, axis=0) - 1
    slot_index = jnp.arange(capacity, dtype=jnp.int32)
    pick_mask = (member[:, :, None] == 1) & (slot_rank[:, :, None] == slot_index[None, None, :])
    selector = pick_mask.reshape(rows_here, exp_count * capacity).T.astype(jnp.bfloat16)
    slot_weight = jnp.sum(jnp.where(pick_mask, gate_of[:, :, None], 0.0), axis=0)
    slot_mixed = jnp.dot(selector, mixed_heads, preferred_element_type=jnp.float32).astype(
        jnp.bfloat16
    )
    row_blocks = jnp.concatenate(
        [mixed_heads.reshape(exp_count, own_rows, -1), slot_mixed.reshape(exp_count, capacity, -1)],
        axis=1,
    )
    stacked = row_blocks.reshape(exp_count * per_block, head_count * head_size)
    pair_rows = jnp.concatenate(by_core(stacked, partner(stacked)), axis=0)
    half_weight = lax.all_gather(out_weight, "yz", axis=1, tiled=True)
    half_width = half_weight.shape[1]
    partial_rows = jnp.dot(pair_rows, half_weight, preferred_element_type=jnp.float32)
    partial_term = partial_rows.astype(jnp.bfloat16).reshape(2, exp_count, per_block, half_width)
    swapped = lax.all_to_all(partial_term, "exp", 1, 1, tiled=True)
    head_sum = jnp.sum(swapped.astype(jnp.float32), axis=1)
    core_here = lax.axis_index("core")
    kept = lax.dynamic_index_in_dim(head_sum, core_here, 0, keepdims=False)
    sent = lax.dynamic_index_in_dim(head_sum, 1 - core_here, 0, keepdims=False)
    by_parity = jnp.stack(by_core(kept, partner(sent)), axis=0)
    block_width = out_weight.shape[1]
    projected = (
        by_parity.reshape(2, per_block, half_width // block_width, block_width)
        .transpose(1, 2, 0, 3)
        .reshape(per_block, model_width)
    )
    stream_own = lax.dynamic_slice_in_dim(stream_in, own_index * own_rows, own_rows, 0)
    own_selector = lax.dynamic_slice_in_dim(selector, own_index * capacity, capacity, 0)
    stream_slots = jnp.dot(own_selector, stream_in, preferred_element_type=jnp.float32)
    residual_rows = jnp.concatenate([stream_own.astype(jnp.float32), stream_slots], axis=0)
    hidden_rows = (residual_rows + projected).astype(jnp.bfloat16)
    residual_out = hidden_rows[:own_rows]
    slot_hidden = hidden_rows[own_rows:]
    outgoing = normalize_rows(slot_hidden, ffn_gain)
    ctx_count = lax.axis_size(CTX)
    chip_rows = jnp.concatenate(by_core(outgoing, partner(outgoing)), axis=0)
    row_piece = lax.all_gather(chip_rows, "yz", axis=0, tiled=True)
    gate_part = jnp.dot(row_piece, w_gate[0], preferred_element_type=jnp.float32)
    up_part = jnp.dot(row_piece, w_up[0], preferred_element_type=jnp.float32)
    activated = (jax.nn.silu(gate_part) * up_part).astype(jnp.bfloat16)
    down_part = jnp.dot(activated, w_down[0], preferred_element_type=jnp.float32)
    down_rows = down_part.astype(jnp.bfloat16).reshape(ctx_count // 2, 2, capacity, model_width)
    down_kept = lax.dynamic_index_in_dim(down_rows, core_here, 1, keepdims=False)
    down_sent = lax.dynamic_index_in_dim(down_rows, 1 - core_here, 1, keepdims=False)
    pair_sum = down_kept.astype(jnp.float32) + partner(down_sent).astype(jnp.float32)
    down_blocks = lax.all_to_all(pair_sum.astype(jnp.bfloat16), "yz", 0, 0, tiled=True)
    summed_down = jnp.sum(down_blocks.astype(jnp.float32), axis=0)
    own_weight = lax.dynamic_index_in_dim(slot_weight, own_index, 0, keepdims=False)
    expert_out = (
        (summed_down * own_weight[:, None])
        .astype(jnp.bfloat16)
        .reshape(1, 1, capacity, model_width)
    )
    return (residual_out, expert_out)


def solution(mesh):
    ctx_size, exp_size = mesh.devices.shape
    split = jax.sharding.Mesh(mesh.devices.reshape(ctx_size // 2, 2, exp_size), ("yz", "core", "exp"))
    return jax.shard_map(
        per_device,
        mesh=split,
        in_specs=(
            P(CTX, None),
            P(CTX, "exp"),
            P(CTX, "exp"),
            P(CTX, "exp"),
            P(CTX, "exp"),
            P("exp"),
            P("exp"),
            P("exp", CTX),
            P(),
            P(CTX, None),
            P(CTX, None),
            P("exp", None, CTX),
            P("exp", None, CTX),
            P("exp", CTX, None),
        ),
        out_specs=(P((CTX[0], CTX[1], "exp"), None), P(CTX, "exp", None, None)),
        check_vma=False,
    )
```

```python
import jax
import jax.numpy as jnp
from jax import lax
from jax.sharding import PartitionSpec as P

HIGHEST = lax.Precision.HIGHEST
CTX = ("yz", "core")


def partner(value):
    return lax.ppermute(value, "core", [(0, 1), (1, 0)])


def by_core(mine, theirs):
    first = lax.axis_index("core") == 0
    return jnp.where(first, mine, theirs), jnp.where(first, theirs, mine)


def decayed_prefix(local_state, decay_rates, rows_here):
    chips = lax.axis_size("yz")
    core_here = lax.axis_index("core")
    half = local_state.shape[0] // 2
    span = jnp.exp(-decay_rates * rows_here)
    other = partner(local_state)
    first_state, second_state = by_core(local_state, other)
    chip_state = span[:, None, None] * first_state + second_state
    my_rates = lax.dynamic_slice_in_dim(decay_rates, core_here * half, half, 0)
    running = lax.dynamic_slice_in_dim(chip_state, core_here * half, half, 0)

    def shift(value, step):
        pairs = [(i, i + step) for i in range(chips - step)]
        return lax.ppermute(value.astype(jnp.bfloat16), "yz", pairs).astype(jnp.float32)

    running = shift(running, 1)
    step = 1
    while step < chips:
        factor = jnp.exp(-my_rates * (2 * rows_here * step))
        running = running + factor[:, None, None] * shift(running, step)
        step *= 2
    mine, theirs = running, partner(running)
    low, high = by_core(mine, theirs)
    chip_prefix = jnp.concatenate([low, high], axis=0)
    return jnp.where(core_here == 0, chip_prefix, span[:, None, None] * chip_prefix + first_state)


def normalize_rows(row_block, ffn_gain):
    wide_rows = row_block.astype(jnp.float32)
    inverse = lax.rsqrt(jnp.mean(wide_rows * wide_rows, axis=1, keepdims=True) + 1e-06)
    return (wide_rows * inverse * ffn_gain[None, :]).astype(jnp.bfloat16)


def per_device(
    stream_in,
    queries,
    key_proj,
    values,
    attn_gate,
    decay_rates,
    attn_gain,
    out_weight,
    ffn_gain,
    routing,
    route_weights,
    w_gate,
    w_up,
    w_down,
):
    rows_here, model_width = stream_in.shape
    head_count = decay_rates.shape[0]
    head_size = queries.shape[1] // head_count
    exp_count = lax.axis_size("exp")
    own_index = lax.axis_index("exp")
    capacity = rows_here // 16
    own_rows = rows_here // exp_count
    per_block = own_rows + capacity
    query_heads = queries.reshape(rows_here, head_count, head_size)
    key_heads = key_proj.reshape(rows_here, head_count, head_size)
    value_heads = values.reshape(rows_here, head_count, head_size)
    positions = jnp.arange(rows_here, dtype=jnp.float32)
    tail_decay = jnp.exp(-decay_rates[None, :] * (rows_here - 1.0 - positions)[:, None])
    weighted_keys = key_heads.astype(jnp.float32) * tail_decay[:, :, None]
    local_state = jnp.einsum(
        "jhd,jhe->hde", weighted_keys, value_heads.astype(jnp.float32), precision=HIGHEST
    )
    prior_state = decayed_prefix(local_state, decay_rates, rows_here)
    scores = jnp.einsum("ihd,jhd->hij", query_heads, key_heads, preferred_element_type=jnp.float32)
    distance = positions[:, None] - positions[None, :]
    decay_mask = jnp.where(
        distance[None] >= 0.0,
        jnp.exp(-decay_rates[:, None, None] * jnp.maximum(distance, 0.0)[None]),
        0.0,
    )
    near_weights = (scores * decay_mask).astype(jnp.bfloat16)
    near_part = jnp.einsum(
        "hij,jhd->ihd", near_weights, value_heads, preferred_element_type=jnp.float32
    )
    lead_decay = jnp.exp(-decay_rates[None, :] * (positions + 1.0)[:, None])
    far_part = jnp.einsum(
        "ihd,hde->ihe",
        query_heads.astype(jnp.float32) * lead_decay[:, :, None],
        prior_state,
        precision=HIGHEST,
    )
    attended = near_part + far_part
    inverse = lax.rsqrt(jnp.mean(attended * attended, axis=2, keepdims=True) + 1e-06)
    normed = (attended * inverse).reshape(rows_here, head_count * head_size)
    mixed_heads = (
        normed * attn_gain[None, :] * jax.nn.sigmoid(attn_gate.astype(jnp.float32))
    ).astype(jnp.bfloat16)
    held_ids = jnp.arange(exp_count, dtype=jnp.int32)
    hit_mask = routing[:, :, None] == held_ids[None, None, :]
    member = jnp.sum(hit_mask.astype(jnp.int32), axis=1)
    gate_of = jnp.sum(jnp.where(hit_mask, route_weights[:, :, None], 0.0), axis=1)
    slot_rank = jnp.cumsum(member, axis=0) - 1
    slot_index = jnp.arange(capacity, dtype=jnp.int32)
    pick_mask = (member[:, :, None] == 1) & (slot_rank[:, :, None] == slot_index[None, None, :])
    selector = pick_mask.reshape(rows_here, exp_count * capacity).T.astype(jnp.bfloat16)
    slot_weight = jnp.sum(jnp.where(pick_mask, gate_of[:, :, None], 0.0), axis=0)
    slot_mixed = jnp.dot(selector, mixed_heads, preferred_element_type=jnp.float32).astype(
        jnp.bfloat16
    )
    core_here = lax.axis_index("core")
    block_width = out_weight.shape[1]
    half_weight = lax.all_gather(out_weight, "yz", axis=1, tiled=True)
    half_width = half_weight.shape[1]
    stream_own = lax.dynamic_slice_in_dim(stream_in, own_index * own_rows, own_rows, 0)
    own_selector = lax.dynamic_slice_in_dim(selector, own_index * capacity, capacity, 0)
    stream_slots = jnp.dot(own_selector, stream_in, preferred_element_type=jnp.float32).astype(
        jnp.bfloat16
    )

    def parity_half(rows, parity):
        shaped = rows.reshape(rows.shape[0], half_width // block_width, 2, block_width)
        return lax.dynamic_index_in_dim(shaped, parity, 2, keepdims=False).reshape(
            rows.shape[0], half_width
        )

    def project(row_block, stream_rows, count):
        pair = jnp.concatenate(by_core(row_block, partner(row_block)), axis=0)
        part = jnp.dot(pair, half_weight, preferred_element_type=jnp.float32)
        part = part.astype(jnp.bfloat16).reshape(2, exp_count, count, half_width)
        head_sum = jnp.sum(lax.all_to_all(part, "exp", 1, 1, tiled=True).astype(jnp.float32), axis=1)
        stream_pair = by_core(
            parity_half(stream_rows, core_here), partner(parity_half(stream_rows, 1 - core_here))
        )
        hidden_half = (jnp.stack(stream_pair, axis=0).astype(jnp.float32) + head_sum).astype(
            jnp.bfloat16
        )
        kept = lax.dynamic_index_in_dim(hidden_half, core_here, 0, keepdims=False)
        sent = lax.dynamic_index_in_dim(hidden_half, 1 - core_here, 0, keepdims=False)
        low, high = by_core(kept, partner(sent))
        shape = (count, half_width // block_width, 1, block_width)
        return jnp.concatenate([low.reshape(shape), high.reshape(shape)], axis=2).reshape(
            count, model_width
        )

    slot_hidden = project(slot_mixed, stream_slots, capacity)
    residual_out = project(mixed_heads, stream_own, own_rows)
    outgoing = normalize_rows(slot_hidden, ffn_gain)
    ctx_count = lax.axis_size(CTX)
    gathered = lax.all_gather(outgoing, "yz", axis=0, tiled=False)
    row_piece = jnp.stack(by_core(gathered, partner(gathered)), axis=1).reshape(
        ctx_count * capacity, model_width
    )
    gate_part = jnp.dot(row_piece, w_gate[0], preferred_element_type=jnp.float32)
    up_part = jnp.dot(row_piece, w_up[0], preferred_element_type=jnp.float32)
    activated = (jax.nn.silu(gate_part) * up_part).astype(jnp.bfloat16)
    down_part = jnp.dot(activated, w_down[0], preferred_element_type=jnp.float32)
    down_rows = down_part.astype(jnp.bfloat16).reshape(ctx_count // 2, 2, capacity, model_width)
    down_kept = lax.dynamic_index_in_dim(down_rows, core_here, 1, keepdims=False)
    down_sent = lax.dynamic_index_in_dim(down_rows, 1 - core_here, 1, keepdims=False)
    pair_sum = down_kept.astype(jnp.float32) + partner(down_sent).astype(jnp.float32)
    down_blocks = lax.all_to_all(pair_sum.astype(jnp.bfloat16), "yz", 0, 0, tiled=True)
    summed_down = jnp.sum(down_blocks.astype(jnp.float32), axis=0)
    own_weight = lax.dynamic_index_in_dim(slot_weight, own_index, 0, keepdims=False)
    expert_out = (
        (summed_down * own_weight[:, None])
        .astype(jnp.bfloat16)
        .reshape(1, 1, capacity, model_width)
    )
    return (residual_out, expert_out)


def solution(mesh):
    ctx_size, exp_size = mesh.devices.shape
    split = jax.sharding.Mesh(mesh.devices.reshape(ctx_size // 2, 2, exp_size), ("yz", "core", "exp"))
    return jax.shard_map(
        per_device,
        mesh=split,
        in_specs=(
            P(CTX, None),
            P(CTX, "exp"),
            P(CTX, "exp"),
            P(CTX, "exp"),
            P(CTX, "exp"),
            P("exp"),
            P("exp"),
            P("exp", CTX),
            P(),
            P(CTX, None),
            P(CTX, None),
            P("exp", None, CTX),
            P("exp", None, CTX),
            P("exp", CTX, None),
        ),
        out_specs=(P((CTX[0], CTX[1], "exp"), None), P(CTX, "exp", None, None)),
        check_vma=False,
    )
```
